32 devices in a mesh: pass: 16 (over z, y, core), voc: 2 (over x).
Axes of the slice: x: 2, y: 2, z: 4, core: 2. Of those that a mesh axis runs over, the one named last changes fastest.
Arguments:
- hidden: bfloat16 [512, 16, 768], P('pass'), may hold values from -6 to 6
- positions: int32 [512, 8], P('pass'), may hold values from 0 to 15
- passage_weight: float32 [512], P('pass'), may hold values from 0.4 to 2.5
- passage_counts: int32 [32], replicated, may hold values from 1 to 24, 512 in all
- passage_slot: int32 [512], replicated, may hold values from 0 to 511, each once
- head_weight: bfloat16 [768, 30720], P(None, 'voc'), may hold values from -0.21875 to 0.21875
- head_bias: float32 [30720], P('voc'), may hold values from -5 to 5
- queries: bfloat16 [32, 30720], P('pass', 'voc'), may hold values from -1 to 1
Outputs:
- scores: float32 [32, 32], P('pass')
- hidden_grad: bfloat16 [512, 16, 768], P('pass')
The draws below stay inside these ranges and needn't reach their ends.
Inputs may be any that keep to these rules, and one draw needn't show every extreme that they name: `passage_slot`: each slot holds exactly one passage.
All inputs are finite; a program needn't handle non-finite values.
Results may differ from the reference program's by a relative error of at most 0.015.
Values may be sent and summed in bfloat16 or wider, within the bound.
No kernel may reach another device: no remote copies, remote signals or barrier semaphores. Data moves between devices by JAX's collectives and lax.ppermute only.
A program may use at most 128 MiB of HBM per device.

```python
import math
import jax
import jax.numpy as jnp
import numpy as np
from jax import lax

D = 768
VOCAB = 30720
SEQ = 16
POS = 8
PASS_DEV = 32
DOC_DEV = 2
PASSAGES = 512
DOCS = 32


def draw_queries(key, part):
    first = jax.random.fold_in(jax.random.fold_in(key, 17), 0)
    per_doc = max(PASS_DEV // DOC_DEV, 1) * 1.0
    spread = 2.0 / (jnp.sqrt(VOCAB * 1.0) * 2.6 * per_doc)
    base = jax.random.normal(first, (DOCS, VOCAB), jnp.float32) * spread
    return base.astype(jnp.bfloat16)


def place_ends(result, stream_key, least, top_value):
    spot = [jax.random.randint(jax.random.fold_in(stream_key, axis), (), 0, length) for axis, length in enumerate(result.shape)]
    longest = result.shape.index(max(result.shape))
    beside = spot[:longest] + [(spot[longest] + 1) % result.shape[longest]] + spot[longest + 1:]
    return result.at[tuple(spot)].set(least).at[tuple(beside)].set(top_value)


def level_of(stream_key, shape, shards, low, high):
    factor_of, own = 1.0, jax.random.fold_in(stream_key, 6)
    for axis_at, shards_of in shards:
        heights = jnp.exp(jax.random.uniform(jax.random.fold_in(own, axis_at), (shards_of,), jnp.float32, low / len(shards), high / len(shards)))
        factor_of = factor_of * jnp.repeat(heights, shape[axis_at] // shards_of).reshape([-1 if axis == axis_at else 1 for axis in range(len(shape))])
    return factor_of


def profile(amount, total, most, skew):
    weights = [(1 << 20) // math.isqrt(standing ** skew) + 1 for standing in range(2, amount + 1)]
    spare, holding = total - most - (amount - 1), [1] * (amount - 1)
    while spare > 0:
        free = [i for i in range(amount - 1) if holding[i] < most]
        mass, left = sum([weights[i] for i in free]), spare
        for i in free:
            more = min(most - holding[i], max(1, left * weights[i] // mass), spare)
            holding[i] = holding[i] + more
            spare = spare - more
    return np.array([most] + holding)


def uneven(own_key, amount, total, limit, lean):
    if amount == 2:
        one = jax.random.randint(own_key, (), max(1, total - limit), min(limit, total - 1) + 1)
        return jnp.stack([one, total - one])
    sizes = jnp.asarray(profile(amount, total, limit, lean), jnp.int32)
    pairs = (amount - 1) // 2
    source_of, receiver = sizes[1:1 + 2 * pairs:2], sizes[2:2 + 2 * pairs:2]
    slack = jnp.minimum(source_of - 1, limit - receiver)
    passed = jax.random.randint(jax.random.fold_in(own_key, 1), (pairs,), 0, 1 << 20) % (slack + 1)
    sizes = sizes.at[1:1 + 2 * pairs:2].set(source_of - passed).at[2:2 + 2 * pairs:2].set(receiver + passed)
    return sizes[jax.random.permutation(jax.random.fold_in(own_key, 2), amount)]


def gaussian(own_key, shape, scale, most, cuts=(), kind=jnp.bfloat16):
    result = scale * jax.random.normal(own_key, shape, jnp.float32)
    if cuts:
        result = result * level_of(own_key, shape, cuts, -0.22, 0.18)
    return jnp.clip(result, -most, most).astype(kind)


def setup_inputs(seed: int = 0) -> dict:
    key_list = jax.random.split(jax.random.key(seed), 9)
    hidden = gaussian(key_list[0], (PASSAGES, SEQ, D), 1.0, 6.0, ((0, 16),))
    positions = place_ends(jax.random.randint(key_list[1], (PASSAGES, POS), 0, SEQ), jax.random.fold_in(key_list[1], 1), 0, SEQ - 1).astype(jnp.int32)
    passage_weight = jnp.clip(jnp.exp(math.log(2.5) - 1.8325814 * jax.random.uniform(key_list[2], (PASSAGES,), jnp.float32) ** level_of(key_list[2], (PASSAGES,), ((0, 16),), -0.2, 0.2)), 0.4, 2.5)
    passage_counts = uneven(key_list[3], DOCS, PASSAGES, 24, 2).astype(jnp.int32)
    passage_slot = jax.random.permutation(key_list[4], PASSAGES).astype(jnp.int32)
    head_weight = gaussian(key_list[5], (D, VOCAB), D ** -0.5, 0.21875, ((1, 2),))
    head_bias = gaussian(key_list[6], (VOCAB,), 1.0, 5.0, ((0, 2),), jnp.float32)
    queries = draw_queries(jax.random.fold_in(key_list[8], 71), 0)
    return {"hidden": hidden, "positions": positions, "passage_weight": passage_weight, "passage_counts": passage_counts, "passage_slot": passage_slot, "head_weight": head_weight, "head_bias": head_bias, "queries": queries}


HIGH = lax.Precision.HIGHEST


def document_of_order(passage_counts):
    ends = jnp.cumsum(passage_counts).astype(jnp.int32)
    order = jnp.arange(PASSAGES, dtype=jnp.int32)
    return jnp.sum((ends[None, :] <= order[:, None]).astype(jnp.int32), axis=1).astype(jnp.int32)


def picked_logits(states, places, head_weight, head_bias):
    picked = jax.vmap(lambda h, p: h[p])(states, places)
    flat = picked.reshape(-1, D)
    return jnp.dot(flat, head_weight, preferred_element_type=jnp.float32) + head_bias.astype(jnp.float32)


def reference(hidden, positions, passage_weight, passage_counts, passage_slot, head_weight, head_bias, queries):
    doc_order = document_of_order(passage_counts)
    doc_slot = jnp.zeros((PASSAGES,), jnp.int32).at[passage_slot].set(doc_order)
    mixing = jnp.where(doc_slot[None, :] == jnp.arange(DOCS, dtype=jnp.int32)[:, None],
                       passage_weight[None, :].astype(jnp.float32), jnp.float32(0.0))
    blocks = PASSAGES // PASS_DEV
    hid_blocks = hidden.reshape(blocks, PASS_DEV, SEQ, D)
    pos_blocks = positions.reshape(blocks, PASS_DEV, POS)

    def forward_block(pair):
        states, places = pair
        logits = picked_logits(states, places, head_weight, head_bias)
        active = jnp.log1p(jnp.maximum(logits, 0.0))
        return active.reshape(PASS_DEV, POS, VOCAB).sum(axis=1).astype(jnp.bfloat16)

    rep = lax.map(forward_block, (hid_blocks, pos_blocks)).reshape(PASSAGES, VOCAB)
    documents = jnp.dot(mixing, rep.astype(jnp.float32), precision=HIGH)
    query_full = queries.astype(jnp.float32)
    scores = jnp.dot(query_full, documents.T, precision=HIGH)
    prob = jax.nn.softmax(scores, axis=1)
    dscore = (prob - jnp.eye(DOCS, dtype=jnp.float32)) / DOCS
    drep = jnp.dot(jnp.dot(mixing.T, dscore.T, precision=HIGH), query_full, precision=HIGH)
    drep_blocks = drep.reshape(blocks, PASS_DEV, VOCAB)

    def backward_block(triple):
        states, places, dblock = triple
        logits = picked_logits(states, places, head_weight, head_bias).reshape(PASS_DEV, POS, VOCAB)
        growth = 1.0 + jnp.maximum(logits, 0.0)
        dlogits = jnp.where(logits > 0, dblock[:, None, :] / growth, jnp.float32(0.0)).astype(jnp.bfloat16)
        dpicked = lax.dot_general(dlogits.reshape(-1, VOCAB), head_weight, (((1,), (1,)), ((), ())),
                                  preferred_element_type=jnp.float32)
        onehot = (places[:, :, None] == jnp.arange(SEQ, dtype=jnp.int32)[None, None, :]).astype(jnp.float32)
        grad = jnp.einsum('bps,bpd->bsd', onehot, dpicked.reshape(PASS_DEV, POS, D), precision=HIGH)
        return grad.astype(jnp.bfloat16)

    hidden_grad = lax.map(backward_block, (hid_blocks, pos_blocks, drep_blocks)).reshape(PASSAGES, SEQ, D)
    return scores, hidden_grad
```

```python
import functools

import jax
import jax.numpy as jnp
from jax import lax
from jax.experimental import pallas as pl
from jax.experimental.pallas import tpu as pltpu
from jax.sharding import PartitionSpec as P

HIGH = lax.Precision.HIGHEST
F32 = jnp.float32
BF16 = jnp.bfloat16
VM = pl.BlockSpec(memory_space=pltpu.VMEM)
HBM = pl.BlockSpec(memory_space=pl.ANY)
MIB = 2**20


def iota(shape, axis):
    return lax.broadcasted_iota(jnp.int32, shape, axis)


def params(limit):
    return pltpu.CompilerParams(vmem_limit_bytes=limit * MIB)


def grid_of(size):
    core = 2 if size % 2 == 0 else 1
    rest = size // core
    inner = 1
    while inner * inner * 4 <= rest and rest % (inner * 2) == 0:
        inner *= 2
    return rest // inner, inner, core


def gather_queries(own, size):
    sizes = grid_of(size)
    strides = (sizes[1] * sizes[2], sizes[2], 1)
    blocks, offsets = own[None], [(0, 0, 0)]

    def moved(value, axis, step):
        n, stride = sizes[axis], strides[axis]
        pairs = []
        for i in range(size):
            at = i // stride % n
            pairs.append((i, i + ((at - step) % n - at) * stride))
        return lax.ppermute(value, "pass", pairs)

    for axis in (1, 0, 2):
        n = sizes[axis]
        plus, minus, got, order = blocks, blocks, [blocks], list(offsets)
        for step in range(1, n // 2 + 1):
            shift = lambda by: [
                tuple(v + by if a == axis else v for a, v in enumerate(o)) for o in offsets
            ]
            if 2 * step == n:
                if n == 2:
                    got.append(moved(plus, axis, 1))
                else:
                    half = plus.shape[0] // 2
                    got.append(moved(plus[:half], axis, 1))
                    got.append(moved(minus[half:], axis, -1))
                order += shift(step)
            else:
                plus = moved(plus, axis, 1)
                minus = moved(minus, axis, -1)
                got += [plus, minus]
                order += shift(step) + shift(-step)
        blocks, offsets = jnp.concatenate(got), order
    place = lax.axis_index("pass")
    here = [place // strides[a] % sizes[a] for a in range(3)]
    table = jnp.array(offsets, jnp.int32)
    rank = sum(((here[a] + table[:, a]) % sizes[a]) * strides[a] for a in range(3))
    return blocks, rank


def pick_kernel(hidden, target, slots, counts, weight, first, picked, mix):
    rows, picks = target.shape
    cells = hidden.shape[0]
    docs = counts.shape[1]
    total = slots.shape[1]
    lane = iota((rows, cells), 1)
    for t in range(picks):
        chosen = (target[:, t : t + 1] == lane).astype(F32).astype(BF16)
        picked[t * rows : (t + 1) * rows, :] = jnp.dot(
            chosen, hidden[...], preferred_element_type=F32
        ).astype(BF16)
    upto = iota((docs, docs), 1) <= iota((docs, docs), 0)
    ends = jnp.sum(jnp.where(upto, counts[...], 0), axis=1, keepdims=True)
    order = jnp.sum((ends <= iota((docs, total), 1)).astype(jnp.int32), axis=0, keepdims=True)
    local = first[0] + iota((rows, total), 0)
    doc = jnp.sum(jnp.where(slots[...] == local, order, 0), axis=1, keepdims=True)
    mix[...] = jnp.where(doc == iota((rows, docs), 1), weight[...], F32(0.0))


def pick(hidden, target, slots, counts, weight, first, picks):
    rows, seq, width = hidden.shape
    docs = counts.shape[0]
    return pl.pallas_call(
        pick_kernel,
        in_specs=[VM, VM, VM, VM, VM, pl.BlockSpec(memory_space=pltpu.SMEM)],
        out_specs=[VM, VM],
        out_shape=[
            jax.ShapeDtypeStruct((rows * picks, width), BF16),
            jax.ShapeDtypeStruct((rows, docs), F32),
        ],
        compiler_params=params(16),
        name="pick",
    )(
        hidden.reshape(rows * seq, width),
        target,
        slots.reshape(1, -1),
        counts.reshape(1, -1),
        weight.reshape(-1, 1),
        first,
    )


def chunk_of(vocab, most):
    best = 128
    for n in range(1, vocab // 128 + 1):
        if vocab % (n * 128) == 0 and n * 128 <= most:
            best = n * 128
    return best


def forward_kernel(picks, step, picked, weight, bias, slope, rep, held, raw, made, in_sem, out_sem):
    vocab = weight.shape[1]
    rows = picked.shape[0] // picks
    count = vocab // step
    span = lambda j: pl.ds(j * step, step)
    loads = [
        pltpu.make_async_copy(weight.at[:, span(j)], held.at[:, span(j)], in_sem.at[j])
        for j in range(count)
    ]
    stores = [
        pltpu.make_async_copy(made.at[:, span(j)], slope.at[:, span(j)], out_sem.at[j])
        for j in range(count)
    ]
    for load in loads:
        load.start()
    for j in range(count + 1):
        if j < count:
            loads[j].wait()
            raw[j % 2] = jnp.dot(
                picked[...], held[:, span(j)], preferred_element_type=F32
            ) + bias[:, span(j)]
        if j > 0:
            at = span(j - 1)
            product = None
            for t in range(picks):
                block = slice(t * rows, (t + 1) * rows)
                logit = raw[(j - 1) % 2, block, :]
                growth = 1.0 + jnp.maximum(logit, 0.0)
                product = growth if t == 0 else product * growth
                made[block, at] = jnp.where(logit > 0, 1.0 / growth, 0.0).astype(BF16)
            rep[:, at] = jnp.log(product).astype(BF16)
            stores[j - 1].start()
    for store in stores:
        store.wait()


def forward(picked, weight, bias, picks):
    cells, width = picked.shape
    vocab = weight.shape[1]
    rows = cells // picks
    step = chunk_of(vocab, 1536)
    count = vocab // step
    return pl.pallas_call(
        functools.partial(forward_kernel, picks, step),
        in_specs=[VM, HBM, VM],
        out_specs=[HBM, VM],
        out_shape=[
            jax.ShapeDtypeStruct((cells, vocab), BF16),
            jax.ShapeDtypeStruct((rows, vocab), BF16),
        ],
        scratch_shapes=[
            pltpu.VMEM((width, vocab), BF16),
            pltpu.VMEM((2, cells, step), F32),
            pltpu.VMEM((cells, vocab), BF16),
            pltpu.SemaphoreType.DMA((count,)),
            pltpu.SemaphoreType.DMA((count,)),
        ],
        cost_estimate=pl.CostEstimate(
            flops=2 * cells * width * vocab,
            transcendentals=0,
            bytes_accessed=2 * width * vocab + 2 * cells * vocab,
        ),
        compiler_params=params(48),
        name="forward",
    )(picked, weight, bias)


def pair_kernel(fold, queries, rep, mix, rank, out):
    docs = mix.shape[1]
    lines = docs // fold
    paired = lax.dot_general(
        queries[...], rep[...], (((1,), (1,)), ((), ())), preferred_element_type=F32
    )
    parts = jnp.dot(paired, mix[...], precision=HIGH, preferred_element_type=F32)
    columns = []
    for m in range(fold):
        chosen = (fold * iota((lines, docs), 0) + m == rank[...]).astype(F32)
        columns.append(jnp.dot(chosen, parts, precision=HIGH, preferred_element_type=F32))
    packed = columns[0] if fold == 1 else jnp.concatenate(columns, axis=1)
    for k in range(out.shape[0]):
        out[k] = packed


def pair(queries, rep, mix, rank, fold, copies):
    docs = mix.shape[1]
    return pl.pallas_call(
        functools.partial(pair_kernel, fold),
        in_specs=[VM] * 4,
        out_specs=VM,
        out_shape=jax.ShapeDtypeStruct((copies, docs // fold, docs * fold), F32),
        compiler_params=params(16),
        name="pair",
    )(queries, rep, mix, rank)


def backward_kernel(
    fold, picks, step, parts, mix, rank, first, queries, slope, weight,
    scores, token, held, made, w_sem, s_sem,
):
    vocab = weight.shape[1]
    rows, docs = mix.shape
    lines = docs // fold
    count = vocab // step
    span = lambda j: pl.ds(j * step, step)
    loads = []
    for j in range(count):
        loads.append(
            (
                pltpu.make_async_copy(slope.at[:, span(j)], made.at[:, span(j)], s_sem.at[j]),
                pltpu.make_async_copy(weight.at[:, span(j)], held.at[:, span(j)], w_sem.at[j]),
            )
        )
        for load in loads[j]:
            load.start()
    packed = parts[0]
    for k in range(1, parts.shape[0]):
        packed = packed + parts[k]
    folded = []
    for m in range(fold):
        folded.append(packed[:, m * docs : (m + 1) * docs])
    score = folded[0] if fold == 1 else jnp.concatenate(folded, axis=0)
    line = iota((docs, 1), 0)
    row = fold * (line % lines) + line // lines
    for k in range(scores.shape[0]):
        scores[k : k + 1, :] = jnp.sum(
            jnp.where(row == first[0] + k, score, 0.0), axis=0, keepdims=True
        )
    top = jnp.max(score, axis=1, keepdims=True)
    raised = jnp.exp(score - top)
    prob = raised / jnp.sum(raised, axis=1, keepdims=True)
    target = (iota((docs, docs), 1) == row).astype(F32)
    dscore = (prob - target) / docs
    by_line = lax.dot_general(
        mix[...], dscore, (((1,), (1,)), ((), ())), precision=HIGH, preferred_element_type=F32
    )
    place = (row == rank[...]).astype(F32)
    factor = jnp.dot(by_line, place, precision=HIGH, preferred_element_type=F32)
    upper = factor.astype(BF16)
    lower = (factor - upper.astype(F32)).astype(BF16)
    both = jnp.concatenate([upper, lower], axis=1)
    for j in range(count):
        at = span(j)
        for load in loads[j]:
            load.wait()
        part = queries[:, at]
        drep = jnp.dot(both, jnp.concatenate([part, part], axis=0), preferred_element_type=F32)
        pieces = []
        for t in range(picks):
            piece = made[t * rows : (t + 1) * rows, at].astype(F32)
            pieces.append((piece * drep).astype(BF16))
        dlogit = jnp.concatenate(pieces, axis=0)
        add = lax.dot_general(
            dlogit, held[:, at], (((1,), (1,)), ((), ())), preferred_element_type=F32
        )
        if j == 0:
            total = add
        else:
            total = total + add
    token[...] = total.astype(BF16)


def backward(parts, mix, rank, first, queries, slope, weight, fold, owned, picks):
    rows, docs = mix.shape
    width, vocab = weight.shape
    step = chunk_of(vocab, 1536)
    count = vocab // step
    return pl.pallas_call(
        functools.partial(backward_kernel, fold, picks, step),
        in_specs=[VM, VM, VM, pl.BlockSpec(memory_space=pltpu.SMEM), VM, HBM, HBM],
        out_specs=[VM, VM],
        out_shape=[
            jax.ShapeDtypeStruct((owned, docs), F32),
            jax.ShapeDtypeStruct((rows * picks, width), BF16),
        ],
        scratch_shapes=[
            pltpu.VMEM((width, vocab), BF16),
            pltpu.VMEM((rows * picks, vocab), BF16),
            pltpu.SemaphoreType.DMA((count,)),
            pltpu.SemaphoreType.DMA((count,)),
        ],
        compiler_params=params(48),
        name="backward",
    )(parts, mix, rank, first, queries, slope, weight)


def place_kernel(target, *refs):
    out = refs[-1]
    cells = target.shape[1]
    spread = (iota((out.shape[0], cells), 0) == target[...]).astype(F32).astype(BF16)
    total = None
    for ref in refs[:-1]:
        part = jnp.dot(spread, ref[...], preferred_element_type=F32)
        total = part if total is None else total + part
    out[...] = total.astype(BF16)


def place(target, tokens, slots):
    width = tokens[0].shape[1]
    return pl.pallas_call(
        place_kernel,
        in_specs=[VM] * (1 + len(tokens)),
        out_specs=VM,
        out_shape=jax.ShapeDtypeStruct((slots, width), BF16),
        compiler_params=params(16),
        name="place",
    )(target, *tokens)


def on_device(sizes, hidden, positions, weight, counts, slots, head_weight, head_bias, queries):
    devices, vocs = sizes
    rows, seq, width = hidden.shape
    picks = positions.shape[1]
    docs = counts.shape[0]
    owned, vocab = queries.shape
    fold = max(1, 128 // docs)
    here = lax.axis_index("pass")
    blocks, block_rank = gather_queries(queries, devices)
    rank = (block_rank[:, None] * owned + jnp.arange(owned, dtype=jnp.int32)).reshape(1, -1)
    first_slot = (here * rows).astype(jnp.int32).reshape(1)
    first_query = (here * owned).astype(jnp.int32).reshape(1)
    target = jnp.arange(rows, dtype=jnp.int32)[:, None] * seq + positions
    picked, mix = pick(hidden, target, slots, counts, weight, first_slot, picks)
    slope, rep = forward(picked, head_weight, head_bias.reshape(1, -1), picks)
    all_queries = blocks.reshape(-1, vocab)
    everyone = devices * vocs
    if everyone * docs * docs * 4 <= MIB:
        parts = pair(all_queries, rep, mix, rank, fold, everyone)
        parts = lax.all_to_all(parts, ("pass", "voc"), 0, 0)
    else:
        parts = pair(all_queries, rep, mix, rank, fold, 1)
        parts = lax.psum(parts, ("pass", "voc"))
    scores, token = backward(
        parts, mix, rank, first_query, all_queries, slope, head_weight, fold, owned, picks
    )
    if vocs == 2:
        tokens = [token, lax.ppermute(token, "voc", [(0, 1), (1, 0)])]
    else:
        tokens = [lax.psum(token, "voc")]
    grad = place(target.T.reshape(1, -1), tokens, rows * seq)
    return scores, grad.reshape(rows, seq, width)


def solution(mesh):
    sizes = (mesh.shape["pass"], mesh.shape["voc"])
    placed = (
        P("pass", None, None),
        P("pass", None),
        P("pass"),
        P(),
        P(),
        P(None, "voc"),
        P("voc"),
        P("pass", "voc"),
    )
    return jax.shard_map(
        functools.partial(on_device, sizes),
        mesh=mesh,
        in_specs=placed,
        out_specs=(P("pass", None), P("pass", None, None)),
        check_vma=False,
    )
```

```python
import functools

import jax
import jax.numpy as jnp
from jax import lax
from jax.experimental import pallas as pl
from jax.experimental.pallas import tpu as pltpu
from jax.sharding import Mesh
from jax.sharding import PartitionSpec as P

HIGH = lax.Precision.HIGHEST
F32 = jnp.float32
BF16 = jnp.bfloat16
VM = pl.BlockSpec(memory_space=pltpu.VMEM)
HBM = pl.BlockSpec(memory_space=pltpu.HBM)
MIB = 2**20


def iota(shape, axis):
    return lax.broadcasted_iota(jnp.int32, shape, axis)


def params(limit):
    return pltpu.CompilerParams(vmem_limit_bytes=limit * MIB)


def grid_of(size):
    core = 2 if size % 2 == 0 else 1
    rest = size // core
    inner = 1
    while inner * inner * 4 <= rest and rest % (inner * 2) == 0:
        inner *= 2
    return rest // inner, inner, core


def in_hbm(value):
    return pltpu.with_memory_space_constraint(value, pltpu.HBM)


def spread_queries(own, sizes):
    size = sizes["outer"] * sizes["inner"]
    sent = jnp.broadcast_to(own[None], (size,) + own.shape)
    return lax.all_to_all(sent, ("outer", "inner"), 0, 0)


def join_queries(mine, cores):
    blocks = [mine]
    for step in range(1, cores):
        pairs = [((i + step) % cores, i) for i in range(cores)]
        blocks.append(lax.ppermute(mine, "core", pairs))
    return blocks


def query_ranks(owned, sizes):
    size, cores = sizes["outer"] * sizes["inner"], sizes["core"]
    here = lax.axis_index("core")
    local = jnp.arange(owned, dtype=jnp.int32)[None, None, :]
    place = jnp.arange(size, dtype=jnp.int32)[None, :, None]
    core = (here + jnp.arange(cores, dtype=jnp.int32)[:, None, None]) % cores
    return ((place * cores + core) * owned + local).reshape(1, -1)


def column_of(row):
    n = row.shape[1]
    eye = iota((n, n), 0) == iota((n, n), 1)
    return jnp.sum(jnp.where(eye, row, jnp.zeros_like(row)), axis=1, keepdims=True)


def picked_rows(hidden, positions, out):
    picks, rows = positions.shape
    cells = hidden.shape[0]
    seq = cells // rows
    lane = iota((rows, cells), 1) - seq * iota((rows, cells), 0)
    for t in range(picks):
        chosen = (column_of(positions[t : t + 1, :]) == lane).astype(F32).astype(BF16)
        out[t * rows : (t + 1) * rows, :] = jnp.dot(
            chosen, hidden[...], preferred_element_type=F32
        ).astype(BF16)


def mixing_of(slots, counts, weight, first, rows):
    docs = counts.shape[1]
    total = slots.shape[1]
    upto = iota((docs, docs), 1) <= iota((docs, docs), 0)
    ends = jnp.sum(jnp.where(upto, counts[...], 0), axis=1, keepdims=True)
    order = jnp.sum((ends <= iota((docs, total), 1)).astype(jnp.int32), axis=0, keepdims=True)
    local = first + iota((rows, total), 0)
    doc = jnp.sum(jnp.where(slots[...] == local, order, 0), axis=1, keepdims=True)
    return jnp.where(doc == iota((rows, docs), 1), column_of(weight[...]), F32(0.0))


def chunk_of(vocab, most):
    best = 128
    for n in range(1, vocab // 128 + 1):
        if vocab % (n * 128) == 0 and n * 128 <= most:
            best = n * 128
    return best


def forward_kernel(
    spans, first, hidden, positions, slots, counts, passage, bias, weight,
    slope, rep, mix,
    hid, pos, slot, count, level, shift, held, made, raw, picked, sems, sem, out_sem,
):
    picks, rows = positions.shape
    smalls = (hidden, positions, slots, counts, passage, bias)
    kept = (hid, pos, slot, count, level, shift)
    early = [
        pltpu.make_async_copy(smalls[k], kept[k], sems.at[k]) for k in range(len(smalls))
    ]
    loads = [
        pltpu.make_async_copy(
            weight.at[:, pl.ds(at, n)], held.at[:, pl.ds(at, n)], sem.at[j]
        )
        for j, (at, n) in enumerate(spans)
    ]
    stores = [
        pltpu.make_async_copy(
            made.at[:, pl.ds(at, n)], slope.at[:, pl.ds(at, n)], out_sem.at[j]
        )
        for j, (at, n) in enumerate(spans)
    ]
    for load in early + loads:
        load.start()
    for load in early:
        load.wait()
    picked_rows(hid, pos, picked)
    mix[...] = mixing_of(slot, count, level, first[0], rows)
    last = len(spans)
    for j in range(last + 1):
        if j < last:
            at, n = spans[j]
            loads[j].wait()
            raw[j % 2, :, :n] = jnp.dot(
                picked[...], held[:, pl.ds(at, n)], preferred_element_type=F32
            ) + shift[:, pl.ds(at, n)]
        if j > 0:
            at, n = spans[j - 1]
            product = None
            for t in range(picks):
                block = slice(t * rows, (t + 1) * rows)
                logit = raw[(j - 1) % 2, block, :n]
                growth = 1.0 + jnp.maximum(logit, 0.0)
                product = growth if t == 0 else product * growth
                made[block, pl.ds(at, n)] = jnp.where(
                    logit > 0, 1.0 / growth, 0.0
                ).astype(BF16)
            rep[:, pl.ds(at, n)] = jnp.log(product).astype(BF16)
            stores[j - 1].start()
    for store in stores:
        store.wait()


def spans_of(vocab, most):
    spans, at = [], 0
    for small in (512, 1024):
        if vocab - at >= small + most:
            spans.append((at, small))
            at += small
    while at < vocab:
        n = min(most, vocab - at)
        spans.append((at, n))
        at += n
    return tuple(spans)


def forward(first, hidden, positions, slots, counts, passage, bias, weight):
    rows, seq, width = hidden.shape
    picks = positions.shape[0]
    vocab = weight.shape[1]
    docs = counts.shape[0]
    cells = rows * picks
    spans = spans_of(vocab, 1536)
    args = (
        hidden.reshape(rows * seq, width),
        positions,
        slots.reshape(1, -1),
        counts.reshape(1, -1),
        passage.reshape(1, -1),
        bias.reshape(1, -1),
    )
    return pl.pallas_call(
        functools.partial(forward_kernel, spans),
        in_specs=[pl.BlockSpec(memory_space=pltpu.SMEM)] + [HBM] * 7,
        out_specs=[HBM, VM, VM],
        out_shape=[
            pltpu.HBM((cells, vocab), BF16),
            jax.ShapeDtypeStruct((rows, vocab), BF16),
            jax.ShapeDtypeStruct((rows, docs), F32),
        ],
        scratch_shapes=[pltpu.VMEM(a.shape, a.dtype) for a in args]
        + [
            pltpu.VMEM((width, vocab), BF16),
            pltpu.VMEM((cells, vocab), BF16),
            pltpu.VMEM((2, cells, max(n for _, n in spans)), F32),
            pltpu.VMEM((cells, width), BF16),
            pltpu.SemaphoreType.DMA((len(args),)),
            pltpu.SemaphoreType.DMA((len(spans),)),
            pltpu.SemaphoreType.DMA((len(spans),)),
        ],
        cost_estimate=pl.CostEstimate(
            flops=2 * cells * width * vocab,
            transcendentals=0,
            bytes_accessed=2 * width * vocab,
        ),
        compiler_params=params(48),
        name="forward",
    )(first, *[in_hbm(a) for a in args], in_hbm(weight))


def pair_kernel(fold, rep, mix, rank, *refs):
    queries, out = refs[:-1], refs[-1]
    docs = mix.shape[1]
    lines = docs // fold
    paired = jnp.concatenate(
        [
            lax.dot_general(
                block[...], rep[...], (((1,), (1,)), ((), ())), preferred_element_type=F32
            )
            for block in queries
        ],
        axis=0,
    )
    parts = jnp.dot(paired, mix[...], precision=HIGH, preferred_element_type=F32)
    columns = []
    for m in range(fold):
        chosen = (fold * iota((lines, docs), 0) + m == rank[...]).astype(F32)
        columns.append(jnp.dot(chosen, parts, precision=HIGH, preferred_element_type=F32))
    packed = columns[0] if fold == 1 else jnp.concatenate(columns, axis=1)
    for k in range(out.shape[0]):
        out[k] = packed


def pair(blocks, rep, mix, rank, fold, copies):
    docs = mix.shape[1]
    return pl.pallas_call(
        functools.partial(pair_kernel, fold),
        in_specs=[VM] * (3 + len(blocks)),
        out_specs=VM,
        out_shape=jax.ShapeDtypeStruct((copies, docs // fold, docs * fold), F32),
        compiler_params=params(8),
        name="pair",
    )(rep, mix, rank, *blocks)


def backward_kernel(fold, step, width, first, parts, mix, rank, slope, weight, *refs):
    queries, (scores, dlogit, token, held, sem, slope_sem) = refs[:-6], refs[-6:]
    loads = []
    for j in range(weight.shape[1] // step):
        at = pl.ds(j * step, step)
        pair_of = (
            pltpu.make_async_copy(slope.at[:, at], dlogit.at[:, at], slope_sem.at[j]),
            pltpu.make_async_copy(weight.at[pl.ds(0, width), at], held.at[:, at], sem.at[j]),
        )
        for load in pair_of:
            load.start()
        loads.append(pair_of)
    vocab = weight.shape[1]
    rows, docs = mix.shape
    lines = docs // fold
    packed = parts[0]
    for k in range(1, parts.shape[0]):
        packed = packed + parts[k]
    folded = [packed[:, m * docs : (m + 1) * docs] for m in range(fold)]
    score = folded[0] if fold == 1 else jnp.concatenate(folded, axis=0)
    line = iota((docs, 1), 0)
    row = fold * (line % lines) + line // lines
    for k in range(scores.shape[0]):
        scores[k : k + 1, :] = jnp.sum(
            jnp.where(row == first[0] + k, score, 0.0), axis=0, keepdims=True
        )
    top = jnp.max(score, axis=1, keepdims=True)
    raised = jnp.exp(score - top)
    prob = raised / jnp.sum(raised, axis=1, keepdims=True)
    target = (iota((docs, docs), 1) == row).astype(F32)
    dscore = (prob - target) / docs
    by_line = lax.dot_general(
        mix[...], dscore, (((1,), (1,)), ((), ())), precision=HIGH, preferred_element_type=F32
    )
    place = (row == rank[...]).astype(F32)
    factor = jnp.dot(by_line, place, precision=HIGH, preferred_element_type=F32)
    upper = factor.astype(BF16)
    lower = (factor - upper.astype(F32)).astype(BF16)
    both = jnp.concatenate([upper, lower], axis=1)
    total = None
    for j in range(vocab // step):
        at = pl.ds(j * step, step)
        part = [block[:, at] for block in queries]
        drep = jnp.dot(both, jnp.concatenate(part + part, axis=0), preferred_element_type=F32)
        for load in loads[j]:
            load.wait()
        for t in range(slope.shape[0] // rows):
            block = slice(t * rows, (t + 1) * rows)
            dlogit[block, at] = (dlogit[block, at].astype(F32) * drep).astype(BF16)
        add = lax.dot_general(
            dlogit[:, at], held[:, at], (((1,), (1,)), ((), ())), preferred_element_type=F32
        )
        total = add if j == 0 else total + add
    token[...] = total.astype(BF16)


def backward(parts, mix, rank, first, blocks, slope, weight, fold, owned, width):
    rows, docs = mix.shape
    cells, vocab = slope.shape
    step = chunk_of(vocab, 1536)
    return pl.pallas_call(
        functools.partial(backward_kernel, fold, step, width),
        in_specs=[pl.BlockSpec(memory_space=pltpu.SMEM)] + [VM] * 3 + [HBM] * 2
        + [VM] * len(blocks),
        out_specs=[VM, VM, VM],
        out_shape=[
            jax.ShapeDtypeStruct((owned, docs), F32),
            pltpu.VMEM((cells, vocab), BF16),
            jax.ShapeDtypeStruct((cells, width), BF16),
        ],
        scratch_shapes=[
            pltpu.VMEM((width, vocab), BF16),
            pltpu.SemaphoreType.DMA((vocab // step,)),
            pltpu.SemaphoreType.DMA((vocab // step,)),
        ],
        cost_estimate=cost(cells, width, vocab),
        compiler_params=params(32),
        name="backward",
    )(first, parts, mix, rank, in_hbm(slope), in_hbm(weight), *blocks)


def cost(cells, width, vocab):
    return pl.CostEstimate(
        flops=2 * cells * width * vocab,
        transcendentals=0,
        bytes_accessed=2 * width * vocab + 2 * cells * vocab,
    )


def rest_kernel(begin, step, dlogit, weight, token, held, sem):
    width = token.shape[1]
    loads = []
    for j in range(weight.shape[1] // step):
        at = pl.ds(j * step, step)
        loads.append(
            pltpu.make_async_copy(weight.at[pl.ds(begin, width), at], held.at[:, at], sem.at[j])
        )
        loads[j].start()
    total = None
    for j, load in enumerate(loads):
        at = pl.ds(j * step, step)
        load.wait()
        add = lax.dot_general(
            dlogit[:, at], held[:, at], (((1,), (1,)), ((), ())), preferred_element_type=F32
        )
        total = add if j == 0 else total + add
    token[...] = total.astype(BF16)


def rest(dlogit, weight, begin, width):
    cells, vocab = dlogit.shape
    step = chunk_of(vocab, 1536)
    return pl.pallas_call(
        functools.partial(rest_kernel, begin, step),
        in_specs=[VM, HBM],
        out_specs=VM,
        out_shape=jax.ShapeDtypeStruct((cells, width), BF16),
        scratch_shapes=[
            pltpu.VMEM((width, vocab), BF16),
            pltpu.SemaphoreType.DMA((vocab // step,)),
        ],
        cost_estimate=cost(cells, width, vocab),
        compiler_params=params(32),
        name="rest",
    )(dlogit, in_hbm(weight))


def place_kernel(copies, positions, *refs):
    out = refs[-1]
    picks, rows = positions.shape
    slots = out.shape[0]
    seq = slots // rows
    cells = positions[...] + seq * iota((picks, rows), 1)
    target = jnp.concatenate([cells[t : t + 1, :] for t in range(picks)], axis=1)
    spread = (iota((slots, rows * picks), 0) == target).astype(F32).astype(BF16)
    begin = 0
    for k in range(0, len(refs) - 1, copies):
        total = None
        for ref in refs[k : k + copies]:
            part = jnp.dot(spread, ref[...], preferred_element_type=F32)
            total = part if total is None else total + part
        width = refs[k].shape[1]
        out[:, begin : begin + width] = total.astype(BF16)
        begin += width


def place(positions, tokens, copies, slots):
    width = sum(t.shape[1] for t in tokens) // copies
    return pl.pallas_call(
        functools.partial(place_kernel, copies),
        in_specs=[VM] * (1 + len(tokens)),
        out_specs=VM,
        out_shape=jax.ShapeDtypeStruct((slots, width), BF16),
        compiler_params=params(8),
        name="place",
    )(positions, *tokens)


def on_device(sizes, hidden, positions, weight, counts, slots, head_weight, head_bias, queries):
    rows, seq, width = hidden.shape
    docs = counts.shape[0]
    owned, vocab = queries.shape
    fold = max(1, 128 // docs)
    vocs = sizes["voc"]
    axes = ("outer", "inner", "core")
    here = lax.axis_index(axes)
    first_slot = (here * rows).astype(jnp.int32).reshape(1)
    first_query = (here * owned).astype(jnp.int32).reshape(1)
    spots = positions.T
    spread = spread_queries(queries, sizes)
    rank = query_ranks(owned, sizes)
    slope, rep, mix = forward(
        first_slot, hidden, spots, slots, counts, weight, head_bias, head_weight
    )
    spread, rep = lax.optimization_barrier((spread, rep))
    blocks = join_queries(spread.reshape(-1, vocab), sizes["core"])
    everyone = sizes["outer"] * sizes["inner"] * sizes["core"] * vocs
    if everyone * docs * docs * 4 <= MIB:
        parts = pair(blocks, rep, mix, rank, fold, everyone)
        parts = lax.all_to_all(parts, axes + ("voc",), 0, 0)
    else:
        parts = pair(blocks, rep, mix, rank, fold, 1)
        parts = lax.psum(parts, axes + ("voc",))
    cut = width // 3 * 2 if width % 384 == 0 else width
    scores, dlogit, token = backward(
        parts, mix, rank, first_query, blocks, slope, head_weight, fold, owned, cut
    )
    pieces = [token]
    if cut < width:
        pieces.append(rest(dlogit, head_weight, cut, width - cut))
    tokens = []
    for token in pieces:
        if vocs == 2:
            tokens += [token, lax.ppermute(token, "voc", [(0, 1), (1, 0)])]
        else:
            tokens.append(lax.psum(token, "voc"))
    copies = 2 if vocs == 2 else 1
    grad = place(spots, tokens, copies, rows * seq)
    return scores, grad.reshape(rows, seq, width)


def solution(mesh):
    outer, inner, core = grid_of(mesh.shape["pass"])
    sizes = {"outer": outer, "inner": inner, "core": core, "voc": mesh.shape["voc"]}
    fine = Mesh(mesh.devices.reshape(tuple(sizes.values())), tuple(sizes))
    whole = ("outer", "inner", "core")
    placed = (
        P(whole, None, None),
        P(whole, None),
        P(whole),
        P(),
        P(),
        P(None, "voc"),
        P("voc"),
        P(whole, "voc"),
    )
    return jax.shard_map(
        functools.partial(on_device, sizes),
        mesh=fine,
        in_specs=placed,
        out_specs=(P(whole, None), P(whole, None, None)),
        check_vma=False,
    )
```

```python
import functools

import jax
import jax.numpy as jnp
from jax import lax
from jax.experimental import pallas as pl
from jax.experimental.pallas import tpu as pltpu
from jax.sharding import Mesh
from jax.sharding import PartitionSpec as P

HIGH = lax.Precision.HIGHEST
F32 = jnp.float32
BF16 = jnp.bfloat16
VM = pl.BlockSpec(memory_space=pltpu.VMEM)
HBM = pl.BlockSpec(memory_space=pltpu.HBM)
MIB = 2**20

AHEAD = 3
FORWARD = (1, 2, 4, 6, 6, 4, 2)
BACKWARD = (1, 2, 2, 2, 2, 1)
REST = (1, 1)


def iota(shape, axis):
    return lax.broadcasted_iota(jnp.int32, shape, axis)


def params(limit):
    return pltpu.CompilerParams(vmem_limit_bytes=limit * MIB)


def grid_of(size):
    core = 2 if size % 2 == 0 else 1
    rest = size // core
    inner = 1
    while inner * inner * 4 <= rest and rest % (inner * 2) == 0:
        inner *= 2
    return rest // inner, inner, core


def in_hbm(value):
    return pltpu.with_memory_space_constraint(value, pltpu.HBM)


def spread_queries(own, sizes):
    size = sizes["outer"] * sizes["inner"]
    sent = jnp.broadcast_to(own[None], (size,) + own.shape)
    return lax.all_to_all(sent, ("outer", "inner"), 0, 0)


def join_queries(mine, cores):
    blocks = [mine]
    for step in range(1, cores):
        pairs = [((i + step) % cores, i) for i in range(cores)]
        blocks.append(lax.ppermute(mine, "core", pairs))
    return blocks


def query_ranks(owned, sizes):
    size, cores = sizes["outer"] * sizes["inner"], sizes["core"]
    here = lax.axis_index("core")
    local = jnp.arange(owned, dtype=jnp.int32)[None, None, :]
    place = jnp.arange(size, dtype=jnp.int32)[None, :, None]
    core = (here + jnp.arange(cores, dtype=jnp.int32)[:, None, None]) % cores
    return ((place * cores + core) * owned + local).reshape(1, -1)


def column_of(row):
    n = row.shape[1]
    eye = iota((n, n), 0) == iota((n, n), 1)
    return jnp.sum(jnp.where(eye, row, jnp.zeros_like(row)), axis=1, keepdims=True)


def picked_rows(hidden, positions, out):
    picks, rows = positions.shape
    cells = hidden.shape[0]
    seq = cells // rows
    lane = iota((rows, cells), 1) - seq * iota((rows, cells), 0)
    for t in range(picks):
        chosen = (column_of(positions[t : t + 1, :]) == lane).astype(F32).astype(BF16)
        out[t * rows : (t + 1) * rows, :] = jnp.dot(
            chosen, hidden[...], preferred_element_type=F32
        ).astype(BF16)


def mixing_of(slots, counts, weight, first, rows):
    docs = counts.shape[1]
    total = slots.shape[1]
    upto = iota((docs, docs), 1) <= iota((docs, docs), 0)
    ends = jnp.sum(jnp.where(upto, counts[...], 0), axis=1, keepdims=True)
    order = jnp.sum((ends <= iota((docs, total), 1)).astype(jnp.int32), axis=0, keepdims=True)
    local = first + iota((rows, total), 0)
    doc = jnp.sum(jnp.where(slots[...] == local, order, 0), axis=1, keepdims=True)
    return jnp.where(doc == iota((rows, docs), 1), column_of(weight[...]), F32(0.0))


def forward_kernel(
    spans, first, hidden, positions, slots, counts, passage, bias, weight,
    slope, rep, mix,
    hid, pos, slot, count, level, shift, held, made, picked, sems, sem, out_sem,
):
    picks, rows = positions.shape
    smalls = (hidden, positions, slots, counts, passage, bias)
    kept = (hid, pos, slot, count, level, shift)
    early = [
        pltpu.make_async_copy(smalls[k], kept[k], sems.at[k]) for k in range(len(smalls))
    ]
    loads = [
        pltpu.make_async_copy(
            weight.at[:, pl.ds(at, n)], held.at[:, pl.ds(at, n)], sem.at[j]
        )
        for j, (at, n) in enumerate(spans)
    ]
    stores = [
        pltpu.make_async_copy(
            made.at[:, pl.ds(at, n)], slope.at[:, pl.ds(at, n)], out_sem.at[j]
        )
        for j, (at, n) in enumerate(spans)
    ]
    for load in early + loads[:AHEAD]:
        load.start()
    for load in early:
        load.wait()
    picked_rows(hid, pos, picked)
    mix[...] = mixing_of(slot, count, level, first[0], rows)
    for j, (begin, whole) in enumerate(spans):
        loads[j].wait()
        if j + AHEAD < len(loads):
            loads[j + AHEAD].start()
        for at in range(begin, begin + whole, 512):
            n = min(512, begin + whole - at)
            logits = jnp.dot(
                picked[...], held[:, pl.ds(at, n)], preferred_element_type=F32
            ) + line_of(shift, at, n)
            growths = 1.0 + jnp.maximum(logits, 0.0)
            made[:, pl.ds(at, n)] = jnp.where(logits > 0, 1.0 / growths, 0.0).astype(BF16)
            product = growths[:rows]
            for t in range(1, picks):
                product = product * growths[t * rows : (t + 1) * rows]
            rep[:, pl.ds(at, n)] = jnp.log(product).astype(BF16)
        stores[j].start()
    for store in stores:
        store.wait()


def line_of(tiles, at, n):
    rows = [tiles[k : k + 1, :] for k in range(at // 128, (at + n) // 128)]
    return jnp.concatenate(rows, axis=1)


def spans_of(vocab, shares):
    unit = 256 if vocab % 256 == 0 else 128
    spans, at, done = [], 0, 0
    for share in shares:
        done += share
        end = vocab // unit * done // sum(shares) * unit
        if end > at:
            spans.append((at, end - at))
            at = end
    return tuple(spans)


def forward(first, hidden, positions, slots, counts, passage, bias, weight):
    rows, seq, width = hidden.shape
    picks = positions.shape[0]
    vocab = weight.shape[1]
    docs = counts.shape[0]
    cells = rows * picks
    spans = spans_of(vocab, FORWARD)
    args = (
        hidden.reshape(rows * seq, width),
        positions,
        slots.reshape(1, -1),
        counts.reshape(1, -1),
        passage.reshape(1, -1),
        bias.reshape(-1, 128),
    )
    return pl.pallas_call(
        functools.partial(forward_kernel, spans),
        in_specs=[pl.BlockSpec(memory_space=pltpu.SMEM)] + [HBM] * 7,
        out_specs=[HBM, VM, VM],
        out_shape=[
            pltpu.HBM((cells, vocab), BF16),
            jax.ShapeDtypeStruct((rows, vocab), BF16),
            jax.ShapeDtypeStruct((rows, docs), F32),
        ],
        scratch_shapes=[pltpu.VMEM(a.shape, a.dtype) for a in args]
        + [
            pltpu.VMEM((width, vocab), BF16),
            pltpu.VMEM((cells, vocab), BF16),
            pltpu.VMEM((cells, width), BF16),
            pltpu.SemaphoreType.DMA((len(args),)),
            pltpu.SemaphoreType.DMA((len(spans),)),
            pltpu.SemaphoreType.DMA((len(spans),)),
        ],
        cost_estimate=pl.CostEstimate(
            flops=2 * cells * width * vocab,
            transcendentals=0,
            bytes_accessed=2 * width * vocab,
        ),
        compiler_params=params(48),
        name="forward",
    )(first, *[in_hbm(a) for a in args], in_hbm(weight))


def pair_kernel(fold, rep, mix, rank, *refs):
    queries, out = refs[:-1], refs[-1]
    docs = mix.shape[1]
    lines = docs // fold
    paired = jnp.concatenate(
        [
            lax.dot_general(
                block[...], rep[...], (((1,), (1,)), ((), ())), preferred_element_type=F32
            )
            for block in queries
        ],
        axis=0,
    )
    parts = jnp.dot(paired, mix[...], precision=HIGH, preferred_element_type=F32)
    columns = []
    for m in range(fold):
        chosen = (fold * iota((lines, docs), 0) + m == rank[...]).astype(F32)
        columns.append(jnp.dot(chosen, parts, precision=HIGH, preferred_element_type=F32))
    packed = columns[0] if fold == 1 else jnp.concatenate(columns, axis=1)
    for k in range(out.shape[0]):
        out[k] = packed


def pair(blocks, rep, mix, rank, fold, copies):
    docs = mix.shape[1]
    return pl.pallas_call(
        functools.partial(pair_kernel, fold),
        in_specs=[VM] * (3 + len(blocks)),
        out_specs=VM,
        out_shape=jax.ShapeDtypeStruct((copies, docs // fold, docs * fold), F32),
        compiler_params=params(8),
        name="pair",
    )(rep, mix, rank, *blocks)


def backward_kernel(fold, spans, width, first, parts, mix, rank, slope, weight, *refs):
    queries, (scores, dlogit, token, held, sem, slope_sem) = refs[:-6], refs[-6:]
    loads = []
    for j, (begin, n) in enumerate(spans):
        at = pl.ds(begin, n)
        pair_of = (
            pltpu.make_async_copy(slope.at[:, at], dlogit.at[:, at], slope_sem.at[j]),
            pltpu.make_async_copy(weight.at[pl.ds(0, width), at], held.at[:, at], sem.at[j]),
        )
        loads.append(pair_of)
    for pair_of in loads[:AHEAD]:
        for load in pair_of:
            load.start()
    vocab = weight.shape[1]
    rows, docs = mix.shape
    lines = docs // fold
    packed = parts[0]
    for k in range(1, parts.shape[0]):
        packed = packed + parts[k]
    folded = [packed[:, m * docs : (m + 1) * docs] for m in range(fold)]
    score = folded[0] if fold == 1 else jnp.concatenate(folded, axis=0)
    line = iota((docs, 1), 0)
    row = fold * (line % lines) + line // lines
    for k in range(scores.shape[0]):
        scores[k : k + 1, :] = jnp.sum(
            jnp.where(row == first[0] + k, score, 0.0), axis=0, keepdims=True
        )
    top = jnp.max(score, axis=1, keepdims=True)
    raised = jnp.exp(score - top)
    prob = raised / jnp.sum(raised, axis=1, keepdims=True)
    target = (iota((docs, docs), 1) == row).astype(F32)
    dscore = (prob - target) / docs
    by_line = lax.dot_general(
        mix[...], dscore, (((1,), (1,)), ((), ())), precision=HIGH, preferred_element_type=F32
    )
    place = (row == rank[...]).astype(F32)
    factor = jnp.dot(by_line, place, precision=HIGH, preferred_element_type=F32)
    upper = factor.astype(BF16)
    lower = (factor - upper.astype(F32)).astype(BF16)
    both = jnp.concatenate([upper, lower], axis=1)
    total = None
    for j, (begin, n) in enumerate(spans):
        at = pl.ds(begin, n)
        part = [block[:, at] for block in queries]
        drep = jnp.dot(both, jnp.concatenate(part + part, axis=0), preferred_element_type=F32)
        for load in loads[j]:
            load.wait()
        if j + AHEAD < len(loads):
            for load in loads[j + AHEAD]:
                load.start()
        for t in range(slope.shape[0] // rows):
            block = slice(t * rows, (t + 1) * rows)
            dlogit[block, at] = (dlogit[block, at].astype(F32) * drep).astype(BF16)
        add = lax.dot_general(
            dlogit[:, at], held[:, at], (((1,), (1,)), ((), ())), preferred_element_type=F32
        )
        total = add if j == 0 else total + add
    token[...] = total.astype(BF16)


def backward(parts, mix, rank, first, blocks, slope, weight, fold, owned, width):
    rows, docs = mix.shape
    cells, vocab = slope.shape
    spans = spans_of(vocab, BACKWARD)
    return pl.pallas_call(
        functools.partial(backward_kernel, fold, spans, width),
        in_specs=[pl.BlockSpec(memory_space=pltpu.SMEM)] + [VM] * 3 + [HBM] * 2
        + [VM] * len(blocks),
        out_specs=[VM, VM, VM],
        out_shape=[
            jax.ShapeDtypeStruct((owned, docs), F32),
            pltpu.VMEM((cells, vocab), BF16),
            jax.ShapeDtypeStruct((cells, width), BF16),
        ],
        scratch_shapes=[
            pltpu.VMEM((width, vocab), BF16),
            pltpu.SemaphoreType.DMA((len(spans),)),
            pltpu.SemaphoreType.DMA((len(spans),)),
        ],
        cost_estimate=cost(cells, width, vocab),
        compiler_params=params(32),
        name="backward",
    )(first, parts, mix, rank, in_hbm(slope), in_hbm(weight), *blocks)


def cost(cells, width, vocab):
    return pl.CostEstimate(
        flops=2 * cells * width * vocab,
        transcendentals=0,
        bytes_accessed=2 * width * vocab + 2 * cells * vocab,
    )


def rest_kernel(begin, spans, dlogit, weight, token, held, sem):
    width = token.shape[1]
    loads = []
    for j, (first, n) in enumerate(spans):
        at = pl.ds(first, n)
        loads.append(
            pltpu.make_async_copy(weight.at[pl.ds(begin, width), at], held.at[:, at], sem.at[j])
        )
    for load in loads[:AHEAD]:
        load.start()
    total = None
    for j, load in enumerate(loads):
        at = pl.ds(*spans[j])
        load.wait()
        if j + AHEAD < len(loads):
            loads[j + AHEAD].start()
        add = lax.dot_general(
            dlogit[:, at], held[:, at], (((1,), (1,)), ((), ())), preferred_element_type=F32
        )
        total = add if j == 0 else total + add
    token[...] = total.astype(BF16)


def rest(dlogit, weight, begin, width):
    cells, vocab = dlogit.shape
    spans = spans_of(vocab, REST)
    return pl.pallas_call(
        functools.partial(rest_kernel, begin, spans),
        in_specs=[VM, HBM],
        out_specs=VM,
        out_shape=jax.ShapeDtypeStruct((cells, width), BF16),
        scratch_shapes=[
            pltpu.VMEM((width, vocab), BF16),
            pltpu.SemaphoreType.DMA((len(spans),)),
        ],
        cost_estimate=cost(cells, width, vocab),
        compiler_params=params(32),
        name="rest",
    )(dlogit, in_hbm(weight))


def place_kernel(copies, positions, *refs):
    out = refs[-1]
    picks, rows = positions.shape
    slots = out.shape[0]
    seq = slots // rows
    cells = positions[...] + seq * iota((picks, rows), 1)
    target = jnp.concatenate([cells[t : t + 1, :] for t in range(picks)], axis=1)
    spread = (iota((slots, rows * picks), 0) == target).astype(F32).astype(BF16)
    begin = 0
    for k in range(0, len(refs) - 1, copies):
        total = None
        for ref in refs[k : k + copies]:
            part = jnp.dot(spread, ref[...], preferred_element_type=F32)
            total = part if total is None else total + part
        width = refs[k].shape[1]
        out[:, begin : begin + width] = total.astype(BF16)
        begin += width


def place(positions, tokens, copies, slots):
    width = sum(t.shape[1] for t in tokens) // copies
    return pl.pallas_call(
        functools.partial(place_kernel, copies),
        in_specs=[VM] * (1 + len(tokens)),
        out_specs=VM,
        out_shape=jax.ShapeDtypeStruct((slots, width), BF16),
        compiler_params=params(8),
        name="place",
    )(positions, *tokens)


def on_device(sizes, hidden, positions, weight, counts, slots, head_weight, head_bias, queries):
    rows, seq, width = hidden.shape
    docs = counts.shape[0]
    owned, vocab = queries.shape
    fold = max(1, 128 // docs)
    vocs = sizes["voc"]
    axes = ("outer", "inner", "core")
    here = lax.axis_index(axes)
    first_slot = (here * rows).astype(jnp.int32).reshape(1)
    first_query = (here * owned).astype(jnp.int32).reshape(1)
    spots = positions.T
    spread = spread_queries(queries, sizes)
    rank = query_ranks(owned, sizes)
    slope, rep, mix = forward(
        first_slot, hidden, spots, slots, counts, weight, head_bias, head_weight
    )
    spread, rep = lax.optimization_barrier((spread, rep))
    blocks = join_queries(spread.reshape(-1, vocab), sizes["core"])
    everyone = sizes["outer"] * sizes["inner"] * sizes["core"] * vocs
    if everyone * docs * docs * 4 <= MIB:
        parts = pair(blocks, rep, mix, rank, fold, everyone)
        parts = lax.all_to_all(parts, axes + ("voc",), 0, 0)
    else:
        parts = pair(blocks, rep, mix, rank, fold, 1)
        parts = lax.psum(parts, axes + ("voc",))
    cut = width // 3 * 2 if width % 384 == 0 else width
    scores, dlogit, token = backward(
        parts, mix, rank, first_query, blocks, slope, head_weight, fold, owned, cut
    )
    pieces = [token]
    if cut < width:
        pieces.append(rest(dlogit, head_weight, cut, width - cut))
    tokens = []
    for token in pieces:
        if vocs == 2:
            tokens += [token, lax.ppermute(token, "voc", [(0, 1), (1, 0)])]
        else:
            tokens.append(lax.psum(token, "voc"))
    copies = 2 if vocs == 2 else 1
    grad = place(spots, tokens, copies, rows * seq)
    return scores, grad.reshape(rows, seq, width)


def solution(mesh):
    outer, inner, core = grid_of(mesh.shape["pass"])
    sizes = {"outer": outer, "inner": inner, "core": core, "voc": mesh.shape["voc"]}
    fine = Mesh(mesh.devices.reshape(tuple(sizes.values())), tuple(sizes))
    whole = ("outer", "inner", "core")
    placed = (
        P(whole, None, None),
        P(whole, None),
        P(whole),
        P(),
        P(),
        P(None, "voc"),
        P("voc"),
        P(whole, "voc"),
    )
    return jax.shard_map(
        functools.partial(on_device, sizes),
        mesh=fine,
        in_specs=placed,
        out_specs=(P(whole, None), P(whole, None, None)),
        check_vma=False,
    )
```

```python
import functools

import jax
import jax.numpy as jnp
from jax import lax
from jax.experimental import pallas as pl
from jax.experimental.pallas import tpu as pltpu
from jax.sharding import Mesh
from jax.sharding import PartitionSpec as P

HIGH = lax.Precision.HIGHEST
F32 = jnp.float32
BF16 = jnp.bfloat16
VM = pl.BlockSpec(memory_space=pltpu.VMEM)
HBM = pl.BlockSpec(memory_space=pltpu.HBM)
MIB = 2**20

AHEAD = 3
KEPT = 2048
FORWARD = (1, 2, 4, 5, 5, 5)
BACKWARD = (2, 3, 3, 2)
REST = (1, 1)


def iota(shape, axis):
    return lax.broadcasted_iota(jnp.int32, shape, axis)


def params(limit):
    return pltpu.CompilerParams(vmem_limit_bytes=limit * MIB)


def grid_of(size):
    core = 2 if size % 2 == 0 else 1
    rest = size // core
    inner = 1
    while inner * inner * 4 <= rest and rest % (inner * 2) == 0:
        inner *= 2
    return rest // inner, inner, core


def in_hbm(value):
    return pltpu.with_memory_space_constraint(value, pltpu.HBM)


def spread_queries(own, sizes):
    size = sizes["outer"] * sizes["inner"]
    sent = jnp.broadcast_to(own[None], (size,) + own.shape)
    return lax.all_to_all(sent, ("outer", "inner"), 0, 0)


def join_queries(mine, cores):
    blocks = [mine]
    for step in range(1, cores):
        pairs = [((i + step) % cores, i) for i in range(cores)]
        blocks.append(lax.ppermute(mine, "core", pairs))
    return blocks


def query_ranks(owned, sizes):
    size, cores = sizes["outer"] * sizes["inner"], sizes["core"]
    here = lax.axis_index("core")
    local = jnp.arange(owned, dtype=jnp.int32)[None, None, :]
    place = jnp.arange(size, dtype=jnp.int32)[None, :, None]
    core = (here + jnp.arange(cores, dtype=jnp.int32)[:, None, None]) % cores
    return ((place * cores + core) * owned + local).reshape(1, -1)


def column_of(row):
    n = row.shape[1]
    eye = iota((n, n), 0) == iota((n, n), 1)
    return jnp.sum(jnp.where(eye, row, jnp.zeros_like(row)), axis=1, keepdims=True)


def picked_rows(hidden, positions, out):
    picks, rows = positions.shape
    cells = hidden.shape[0]
    seq = cells // rows
    lane = iota((rows, cells), 1) - seq * iota((rows, cells), 0)
    for t in range(picks):
        chosen = (column_of(positions[t : t + 1, :]) == lane).astype(F32).astype(BF16)
        out[t * rows : (t + 1) * rows, :] = jnp.dot(
            chosen, hidden[...], preferred_element_type=F32
        ).astype(BF16)


def mixing_of(slots, counts, weight, first, rows):
    docs = counts.shape[1]
    total = slots.shape[1]
    upto = iota((docs, docs), 1) <= iota((docs, docs), 0)
    ends = jnp.sum(jnp.where(upto, counts[...], 0), axis=1, keepdims=True)
    order = jnp.sum((ends <= iota((docs, total), 1)).astype(jnp.int32), axis=0, keepdims=True)
    local = first + iota((rows, total), 0)
    doc = jnp.sum(jnp.where(slots[...] == local, order, 0), axis=1, keepdims=True)
    return jnp.where(doc == iota((rows, docs), 1), column_of(weight[...]), F32(0.0))


def forward_kernel(
    spans, first, hidden, positions, slots, counts, passage, bias, weight,
    slope, kept_slope, rep, mix,
    hid, pos, slot, count, level, shift, held, made, picked, sems, sem, out_sem,
):
    picks, rows = positions.shape
    smalls = (hidden, positions, slots, counts, passage, bias)
    kept = (hid, pos, slot, count, level, shift)
    early = [
        pltpu.make_async_copy(smalls[k], kept[k], sems.at[k]) for k in range(len(smalls))
    ]
    loads = [
        pltpu.make_async_copy(
            weight.at[:, pl.ds(at, n)], held.at[:, pl.ds(at, n)], sem.at[j]
        )
        for j, (at, n) in enumerate(spans)
    ]
    out = slope.shape[1]
    stores = [
        pltpu.make_async_copy(
            made.at[:, pl.ds(at, n)], slope.at[:, pl.ds(at, n)], out_sem.at[j]
        )
        for j, (at, n) in enumerate(spans)
        if at < out
    ]
    for load in early + loads[:AHEAD]:
        load.start()
    for load in early:
        load.wait()
    picked_rows(hid, pos, picked)
    mix[...] = mixing_of(slot, count, level, first[0], rows)
    for j, (begin, whole) in enumerate(spans):
        loads[j].wait()
        if j + AHEAD < len(loads):
            loads[j + AHEAD].start()
        for at in range(begin, begin + whole, 512):
            n = min(512, begin + whole - at)
            logits = jnp.dot(
                picked[...], held[:, pl.ds(at, n)], preferred_element_type=F32
            ) + line_of(shift, at, n)
            growths = 1.0 + jnp.maximum(logits, 0.0)
            steep = jnp.where(logits > 0, 1.0 / growths, 0.0).astype(BF16)
            if at < out:
                made[:, pl.ds(at, n)] = steep
            else:
                kept_slope[:, pl.ds(at - out, n)] = steep
            product = growths[:rows]
            for t in range(1, picks):
                product = product * growths[t * rows : (t + 1) * rows]
            rep[:, pl.ds(at, n)] = jnp.log(product).astype(BF16)
        if begin < out:
            stores[j].start()
    for store in stores:
        store.wait()


def line_of(tiles, at, n):
    rows = [tiles[k : k + 1, :] for k in range(at // 128, (at + n) // 128)]
    return jnp.concatenate(rows, axis=1)


def spans_of(vocab, shares):
    unit = 256 if vocab % 256 == 0 else 128
    spans, at, done = [], 0, 0
    for share in shares:
        done += share
        end = vocab // unit * done // sum(shares) * unit
        if end > at:
            spans.append((at, end - at))
            at = end
    return tuple(spans)


def forward(first, hidden, positions, slots, counts, passage, bias, weight):
    rows, seq, width = hidden.shape
    picks = positions.shape[0]
    vocab = weight.shape[1]
    docs = counts.shape[0]
    cells = rows * picks
    keep = KEPT if vocab % 512 == 0 and vocab >= 4 * KEPT else 512
    spans = spans_of(vocab - keep, FORWARD) + ((vocab - keep, keep),)
    args = (
        hidden.reshape(rows * seq, width),
        positions,
        slots.reshape(1, -1),
        counts.reshape(1, -1),
        passage.reshape(1, -1),
        bias.reshape(-1, 128),
    )
    return pl.pallas_call(
        functools.partial(forward_kernel, spans),
        in_specs=[pl.BlockSpec(memory_space=pltpu.SMEM)] + [HBM] * 7,
        out_specs=[HBM, VM, VM, VM],
        out_shape=[
            pltpu.HBM((cells, vocab - keep), BF16),
            pltpu.VMEM((cells, keep), BF16),
            jax.ShapeDtypeStruct((rows, vocab), BF16),
            jax.ShapeDtypeStruct((rows, docs), F32),
        ],
        scratch_shapes=[pltpu.VMEM(a.shape, a.dtype) for a in args]
        + [
            pltpu.VMEM((width, vocab), BF16),
            pltpu.VMEM((cells, vocab - keep), BF16),
            pltpu.VMEM((cells, width), BF16),
            pltpu.SemaphoreType.DMA((len(args),)),
            pltpu.SemaphoreType.DMA((len(spans),)),
            pltpu.SemaphoreType.DMA((len(spans),)),
        ],
        cost_estimate=pl.CostEstimate(
            flops=2 * cells * width * vocab,
            transcendentals=0,
            bytes_accessed=2 * width * vocab,
        ),
        compiler_params=params(48),
        name="forward",
    )(first, *[in_hbm(a) for a in args], in_hbm(weight))


def near_kernel(rep, block, out):
    out[...] = lax.dot_general(
        block[...], rep[...], (((1,), (1,)), ((), ())), preferred_element_type=F32
    )


def near(block, rep):
    rows, vocab = block.shape
    return pl.pallas_call(
        near_kernel,
        in_specs=[VM, VM],
        out_specs=VM,
        out_shape=jax.ShapeDtypeStruct((rows, rep.shape[0]), F32),
        cost_estimate=cost(rows, rep.shape[0], vocab),
        compiler_params=params(8),
        name="near",
    )(rep, block)


def pair_kernel(fold, rep, mix, rank, first, *refs):
    queries, out = refs[:-1], refs[-1]
    docs = mix.shape[1]
    lines = docs // fold
    paired = jnp.concatenate(
        [first[...]]
        + [
            lax.dot_general(
                block[...], rep[...], (((1,), (1,)), ((), ())), preferred_element_type=F32
            )
            for block in queries
        ],
        axis=0,
    )
    parts = jnp.dot(paired, mix[...], precision=HIGH, preferred_element_type=F32)
    line = iota((docs, 1), 0)
    chosen = (fold * (line % lines) + line // lines == rank[...]).astype(F32)
    ordered = jnp.dot(chosen, parts, precision=HIGH, preferred_element_type=F32)
    columns = [ordered[m * lines : (m + 1) * lines, :] for m in range(fold)]
    packed = columns[0] if fold == 1 else jnp.concatenate(columns, axis=1)
    for k in range(out.shape[0]):
        out[k] = packed


def pair(blocks, rep, mix, rank, fold, copies):
    docs = mix.shape[1]
    return pl.pallas_call(
        functools.partial(pair_kernel, fold),
        in_specs=[VM] * (3 + len(blocks)),
        out_specs=VM,
        out_shape=jax.ShapeDtypeStruct((copies, docs // fold, docs * fold), F32),
        compiler_params=params(8),
        name="pair",
    )(rep, mix, rank, near(blocks[0], rep), *blocks[1:])


def backward_kernel(fold, spans, width, first, parts, mix, rank, slope, kept_slope, weight, *refs):
    queries, (scores, dlogit, token, held, sem, slope_sem) = refs[:-6], refs[-6:]
    loads = []
    for j, (begin, n) in enumerate(spans):
        at = pl.ds(begin, n)
        pair_of = [pltpu.make_async_copy(weight.at[pl.ds(0, width), at], held.at[:, at], sem.at[j])]
        if begin < slope.shape[1]:
            pair_of.append(
                pltpu.make_async_copy(slope.at[:, at], dlogit.at[:, at], slope_sem.at[j])
            )
        loads.append(pair_of)
    for pair_of in loads[:AHEAD]:
        for load in pair_of:
            load.start()
    vocab = weight.shape[1]
    rows, docs = mix.shape
    lines = docs // fold
    packed = parts[0]
    for k in range(1, parts.shape[0]):
        packed = packed + parts[k]
    folded = [packed[:, m * docs : (m + 1) * docs] for m in range(fold)]
    score = folded[0] if fold == 1 else jnp.concatenate(folded, axis=0)
    line = iota((docs, 1), 0)
    row = fold * (line % lines) + line // lines
    for k in range(scores.shape[0]):
        scores[k : k + 1, :] = jnp.sum(
            jnp.where(row == first[0] + k, score, 0.0), axis=0, keepdims=True
        )
    top = jnp.max(score, axis=1, keepdims=True)
    raised = jnp.exp(score - top)
    prob = raised / jnp.sum(raised, axis=1, keepdims=True)
    target = (iota((docs, docs), 1) == row).astype(F32)
    dscore = (prob - target) / docs
    by_line = lax.dot_general(
        mix[...], dscore, (((1,), (1,)), ((), ())), precision=HIGH, preferred_element_type=F32
    )
    place = (row == rank[...]).astype(F32)
    factor = jnp.dot(by_line, place, precision=HIGH, preferred_element_type=F32)
    upper = factor.astype(BF16)
    lower = (factor - upper.astype(F32)).astype(BF16)
    both = jnp.concatenate([upper, lower], axis=1)
    total = None
    for j, (begin, n) in enumerate(spans):
        at = pl.ds(begin, n)
        part = [block[:, at] for block in queries]
        drep = jnp.dot(both, jnp.concatenate(part + part, axis=0), preferred_element_type=F32)
        for load in loads[j]:
            load.wait()
        if j + AHEAD < len(loads):
            for load in loads[j + AHEAD]:
                load.start()
        for t in range(slope.shape[0] // rows):
            block = slice(t * rows, (t + 1) * rows)
            if begin < slope.shape[1]:
                steep = dlogit[block, at]
            else:
                steep = kept_slope[block, pl.ds(begin - slope.shape[1], n)]
            dlogit[block, at] = (steep.astype(F32) * drep).astype(BF16)
        add = lax.dot_general(
            dlogit[:, at], held[:, at], (((1,), (1,)), ((), ())), preferred_element_type=F32
        )
        total = add if j == 0 else total + add
    token[...] = total.astype(BF16)


def backward(parts, mix, rank, first, blocks, slope, kept_slope, weight, fold, owned, width):
    rows, docs = mix.shape
    cells = slope.shape[0]
    vocab = weight.shape[1]
    out = slope.shape[1]
    spans = ((out, vocab - out),) + spans_of(out, BACKWARD)
    return pl.pallas_call(
        functools.partial(backward_kernel, fold, spans, width),
        in_specs=[pl.BlockSpec(memory_space=pltpu.SMEM)] + [VM] * 3 + [HBM, VM, HBM]
        + [VM] * len(blocks),
        out_specs=[VM, VM, VM],
        out_shape=[
            jax.ShapeDtypeStruct((owned, docs), F32),
            pltpu.VMEM((cells, vocab), BF16),
            jax.ShapeDtypeStruct((cells, width), BF16),
        ],
        scratch_shapes=[
            pltpu.VMEM((width, vocab), BF16),
            pltpu.SemaphoreType.DMA((len(spans),)),
            pltpu.SemaphoreType.DMA((len(spans),)),
        ],
        cost_estimate=cost(cells, width, vocab),
        compiler_params=params(32),
        name="backward",
    )(first, parts, mix, rank, in_hbm(slope), kept_slope, in_hbm(weight), *blocks)


def cost(cells, width, vocab):
    return pl.CostEstimate(
        flops=2 * cells * width * vocab,
        transcendentals=0,
        bytes_accessed=2 * width * vocab + 2 * cells * vocab,
    )


def rest_kernel(begin, spans, dlogit, weight, token, held, sem):
    width = token.shape[1]
    loads = []
    for j, (first, n) in enumerate(spans):
        at = pl.ds(first, n)
        loads.append(
            pltpu.make_async_copy(weight.at[pl.ds(begin, width), at], held.at[:, at], sem.at[j])
        )
    for load in loads[:AHEAD]:
        load.start()
    total = None
    for j, load in enumerate(loads):
        at = pl.ds(*spans[j])
        load.wait()
        if j + AHEAD < len(loads):
            loads[j + AHEAD].start()
        add = lax.dot_general(
            dlogit[:, at], held[:, at], (((1,), (1,)), ((), ())), preferred_element_type=F32
        )
        total = add if j == 0 else total + add
    token[...] = total.astype(BF16)


def rest(dlogit, weight, begin, width):
    cells, vocab = dlogit.shape
    spans = spans_of(vocab, REST)
    return pl.pallas_call(
        functools.partial(rest_kernel, begin, spans),
        in_specs=[VM, HBM],
        out_specs=VM,
        out_shape=jax.ShapeDtypeStruct((cells, width), BF16),
        scratch_shapes=[
            pltpu.VMEM((width, vocab), BF16),
            pltpu.SemaphoreType.DMA((len(spans),)),
        ],
        cost_estimate=cost(cells, width, vocab),
        compiler_params=params(32),
        name="rest",
    )(dlogit, in_hbm(weight))


def place_kernel(copies, begin, positions, *refs):
    tokens, (out, made, sem) = refs[:copies], refs[-3:]
    picks, rows = positions.shape
    slots, width = made.shape
    seq = slots // rows
    cells = positions[...] + seq * iota((picks, rows), 1)
    target = jnp.concatenate([cells[t : t + 1, :] for t in range(picks)], axis=1)
    spread = (iota((slots, rows * picks), 0) == target).astype(F32).astype(BF16)
    total = None
    for ref in tokens:
        part = jnp.dot(spread, ref[...], preferred_element_type=F32)
        total = part if total is None else total + part
    made[...] = total.astype(BF16)
    copy = pltpu.make_async_copy(made, out.at[:, pl.ds(begin, width)], sem)
    copy.start()
    copy.wait()


def place(positions, tokens, begin, before, slots, width):
    part = tokens[0].shape[1]
    given = [] if before is None else [before]
    return pl.pallas_call(
        functools.partial(place_kernel, len(tokens), begin),
        in_specs=[VM] * (1 + len(tokens)) + [HBM] * len(given),
        out_specs=HBM,
        out_shape=pltpu.HBM((slots, width), BF16),
        scratch_shapes=[pltpu.VMEM((slots, part), BF16), pltpu.SemaphoreType.DMA(())],
        input_output_aliases={1 + len(tokens): 0} if given else {},
        cost_estimate=cost(slots, part, tokens[0].shape[0]),
        compiler_params=params(8),
        name="place",
    )(positions, *tokens, *given)


def on_device(sizes, hidden, positions, weight, counts, slots, head_weight, head_bias, queries):
    rows, seq, width = hidden.shape
    docs = counts.shape[0]
    owned, vocab = queries.shape
    fold = max(1, 128 // docs)
    vocs = sizes["voc"]
    axes = ("outer", "inner", "core")
    here = lax.axis_index(axes)
    first_slot = (here * rows).astype(jnp.int32).reshape(1)
    first_query = (here * owned).astype(jnp.int32).reshape(1)
    spots = positions.T
    spread = spread_queries(queries, sizes)
    rank = query_ranks(owned, sizes)
    slope, kept_slope, rep, mix = forward(
        first_slot, hidden, spots, slots, counts, weight, head_bias, head_weight
    )
    spread, rep = lax.optimization_barrier((spread, rep))
    blocks = join_queries(spread.reshape(-1, vocab), sizes["core"])
    everyone = sizes["outer"] * sizes["inner"] * sizes["core"] * vocs
    if everyone * docs * docs * 4 <= MIB:
        parts = pair(blocks, rep, mix, rank, fold, everyone)
        parts = lax.all_to_all(parts, axes + ("voc",), 0, 0)
    else:
        parts = pair(blocks, rep, mix, rank, fold, 1)
        parts = lax.psum(parts, axes + ("voc",))
    cut = width // 3 * 2 if width % 384 == 0 else width
    scores, dlogit, token = backward(
        parts, mix, rank, first_query, blocks, slope, kept_slope, head_weight,
        fold, owned, cut,
    )
    pieces = [token]
    if cut < width:
        pieces.append(rest(dlogit, head_weight, cut, width - cut))
    grad, begin = None, 0
    for token in pieces:
        if vocs == 2:
            tokens = [token, lax.ppermute(token, "voc", [(0, 1), (1, 0)])]
        else:
            tokens = [lax.psum(token, "voc")]
        grad = place(spots, tokens, begin, grad, rows * seq, width)
        begin += token.shape[1]
    return scores, grad.reshape(rows, seq, width)


def solution(mesh):
    outer, inner, core = grid_of(mesh.shape["pass"])
    sizes = {"outer": outer, "inner": inner, "core": core, "voc": mesh.shape["voc"]}
    fine = Mesh(mesh.devices.reshape(tuple(sizes.values())), tuple(sizes))
    whole = ("outer", "inner", "core")
    placed = (
        P(whole, None, None),
        P(whole, None),
        P(whole),
        P(),
        P(),
        P(None, "voc"),
        P("voc"),
        P(whole, "voc"),
    )
    return jax.shard_map(
        functools.partial(on_device, sizes),
        mesh=fine,
        in_specs=placed,
        out_specs=(P(whole, None), P(whole, None, None)),
        check_vma=False,
    )
```

```python
import functools

import jax
import jax.numpy as jnp
from jax import lax
from jax.experimental import pallas as pl
from jax.experimental.pallas import tpu as pltpu
from jax.sharding import Mesh
from jax.sharding import PartitionSpec as P

HIGH = lax.Precision.HIGHEST
F32 = jnp.float32
BF16 = jnp.bfloat16
VM = pl.BlockSpec(memory_space=pltpu.VMEM)
HBM = pl.BlockSpec(memory_space=pltpu.HBM)
MIB = 2**20

AHEAD = 3
KEPT = 2048
FORWARD = (3, 7, 12, 12, 12)
BACKWARD = (1, 2, 2, 2, 1)
REST = (2, 3)


def iota(shape, axis):
    return lax.broadcasted_iota(jnp.int32, shape, axis)


def params(limit):
    return pltpu.CompilerParams(vmem_limit_bytes=limit * MIB)


def grid_of(size):
    core = 2 if size % 2 == 0 else 1
    rest = size // core
    inner = 1
    while inner * inner * 4 <= rest and rest % (inner * 2) == 0:
        inner *= 2
    return rest // inner, inner, core


def in_hbm(value):
    return pltpu.with_memory_space_constraint(value, pltpu.HBM)


def join_queries(mine, cores):
    blocks = [mine]
    for step in range(1, cores):
        pairs = [((i + step) % cores, i) for i in range(cores)]
        blocks.append(lax.ppermute(mine, "core", pairs))
    return blocks


def query_ranks(owned, sizes):
    size, cores = sizes["outer"] * sizes["inner"], sizes["core"]
    here = lax.axis_index("core")
    local = jnp.arange(owned, dtype=jnp.int32)[None, None, :]
    place = jnp.arange(size, dtype=jnp.int32)[None, :, None]
    core = (here + jnp.arange(cores, dtype=jnp.int32)[:, None, None]) % cores
    return ((place * cores + core) * owned + local).reshape(1, -1)


def column_of(row):
    n = row.shape[1]
    eye = iota((n, n), 0) == iota((n, n), 1)
    return jnp.sum(jnp.where(eye, row, jnp.zeros_like(row)), axis=1, keepdims=True)


def picked_rows(hidden, positions, out):
    picks, rows = positions.shape
    cells = hidden.shape[0]
    seq = cells // rows
    lane = iota((rows, cells), 1) - seq * iota((rows, cells), 0)
    for t in range(picks):
        chosen = (column_of(positions[t : t + 1, :]) == lane).astype(F32).astype(BF16)
        out[t * rows : (t + 1) * rows, :] = jnp.dot(
            chosen, hidden[...], preferred_element_type=F32
        ).astype(BF16)


def mixing_of(slots, counts, weight, first, rows):
    docs = counts.shape[1]
    total = slots.shape[1]
    upto = iota((docs, docs), 1) <= iota((docs, docs), 0)
    ends = jnp.sum(jnp.where(upto, counts[...], 0), axis=1, keepdims=True)
    order = jnp.sum((ends <= iota((docs, total), 1)).astype(jnp.int32), axis=0, keepdims=True)
    local = first + iota((rows, total), 0)
    doc = jnp.sum(jnp.where(slots[...] == local, order, 0), axis=1, keepdims=True)
    return jnp.where(doc == iota((rows, docs), 1), column_of(weight[...]), F32(0.0))


def ready_kernel(
    first, own, hidden, positions, slots, counts, passage, bias, weight,
    sent, picked, mix, shift, lead,
    mine, hid, pos, slot, count, level, sems, sent_sems,
):
    rows = positions.shape[1]
    sources = (own, positions, slots, counts, passage, hidden, bias)
    targets = (mine, pos, slot, count, level, hid, shift)
    loads = [pltpu.make_async_copy(sources[k], targets[k], sems.at[k]) for k in range(7)]
    loads.append(pltpu.make_async_copy(weight.at[:, pl.ds(0, lead.shape[1])], lead, sems.at[7]))
    sends = [pltpu.make_async_copy(mine, sent.at[k], sent_sems.at[k]) for k in range(sent.shape[0])]
    for load in loads:
        load.start()
    loads[0].wait()
    for send in sends:
        send.start()
    for load in loads[1:6]:
        load.wait()
    picked_rows(hid, pos, picked)
    mix[...] = mixing_of(slot, count, level, first[0], rows)
    for copy in loads[6:] + sends:
        copy.wait()


def ready(first, own, hidden, positions, slots, counts, passage, bias, weight, copies, lead):
    rows, seq, width = hidden.shape
    picks = positions.shape[0]
    docs = counts.shape[0]
    args = (
        own,
        hidden.reshape(rows * seq, width),
        positions,
        slots.reshape(1, -1),
        counts.reshape(1, -1),
        passage.reshape(1, -1),
        bias.reshape(-1, 128),
    )
    return pl.pallas_call(
        ready_kernel,
        in_specs=[pl.BlockSpec(memory_space=pltpu.SMEM)] + [HBM] * 8,
        out_specs=[HBM] + [VM] * 4,
        out_shape=[
            pltpu.HBM((copies,) + own.shape, own.dtype),
            pltpu.VMEM((rows * picks, width), BF16),
            pltpu.VMEM((rows, docs), F32),
            pltpu.VMEM(args[6].shape, F32),
            pltpu.VMEM((width, lead), BF16),
        ],
        scratch_shapes=[pltpu.VMEM(a.shape, a.dtype) for a in args[:6]]
        + [pltpu.SemaphoreType.DMA((8,)), pltpu.SemaphoreType.DMA((copies,))],
        compiler_params=params(8),
        name="ready",
    )(first, *[in_hbm(a) for a in args], in_hbm(weight))


def forward_kernel(
    spans, picked, shift, lead, weight, slope, kept_slope, rep, held, made, sem, out_sem
):
    rows = rep.shape[0]
    picks = picked.shape[0] // rows
    out = slope.shape[1]
    ready_to = lead.shape[1]
    loads = [
        pltpu.make_async_copy(weight.at[:, pl.ds(at, n)], held.at[:, pl.ds(at, n)], sem.at[j])
        for j, (at, n) in enumerate(spans)
        if at >= ready_to
    ]
    stores = [
        pltpu.make_async_copy(made.at[:, pl.ds(at, n)], slope.at[:, pl.ds(at, n)], out_sem.at[j])
        for j, (at, n) in enumerate(spans)
        if at < out
    ]
    for load in loads[:AHEAD]:
        load.start()
    for j, (begin, whole) in enumerate(spans):
        source = held if begin >= ready_to else lead
        if j > 0:
            loads[j - 1].wait()
            if j - 1 + AHEAD < len(loads):
                loads[j - 1 + AHEAD].start()
        for at in range(begin, begin + whole, 512):
            n = min(512, begin + whole - at)
            logits = jnp.dot(
                picked[...], source[:, pl.ds(at, n)], preferred_element_type=F32
            ) + line_of(shift, at, n)
            growths = 1.0 + jnp.maximum(logits, 0.0)
            steep = jnp.where(logits > 0, 1.0 / growths, 0.0).astype(BF16)
            if at < out:
                made[:, pl.ds(at, n)] = steep
            else:
                kept_slope[:, pl.ds(at - out, n)] = steep
            product = growths[:rows]
            for t in range(1, picks):
                product = product * growths[t * rows : (t + 1) * rows]
            rep[:, pl.ds(at, n)] = jnp.log(product).astype(BF16)
        if begin < out:
            stores[j].start()
    for store in stores:
        store.wait()


def line_of(tiles, at, n):
    rows = [tiles[k : k + 1, :] for k in range(at // 128, (at + n) // 128)]
    return jnp.concatenate(rows, axis=1)


def spans_of(vocab, shares):
    unit = 256 if vocab % 256 == 0 else 128
    spans, at, done = [], 0, 0
    for share in shares:
        done += share
        end = vocab // unit * done // sum(shares) * unit
        if end > at:
            spans.append((at, end - at))
            at = end
    return tuple(spans)


def forward(picked, shift, lead, weight, rows):
    width, vocab = weight.shape
    cells = picked.shape[0]
    begin = lead.shape[1]
    keep = KEPT if vocab % 512 == 0 and vocab >= 4 * KEPT else 512
    middle = spans_of(vocab - keep - begin, FORWARD)
    spans = ((0, begin),) + tuple((begin + at, n) for at, n in middle)
    spans += ((vocab - keep, keep),)
    return pl.pallas_call(
        functools.partial(forward_kernel, spans),
        in_specs=[VM, VM, VM, HBM],
        out_specs=[HBM, VM, VM],
        out_shape=[
            pltpu.HBM((cells, vocab - keep), BF16),
            pltpu.VMEM((cells, keep), BF16),
            jax.ShapeDtypeStruct((rows, vocab), BF16),
        ],
        scratch_shapes=[
            pltpu.VMEM((width, vocab), BF16),
            pltpu.VMEM((cells, vocab - keep), BF16),
            pltpu.SemaphoreType.DMA((len(spans),)),
            pltpu.SemaphoreType.DMA((len(spans),)),
        ],
        cost_estimate=cost(cells, width, vocab),
        compiler_params=params(48),
        name="forward",
    )(picked, shift, lead, in_hbm(weight))


def near_kernel(rep, block, out):
    out[...] = lax.dot_general(
        block[...], rep[...], (((1,), (1,)), ((), ())), preferred_element_type=F32
    )


def near(block, rep):
    rows, vocab = block.shape
    return pl.pallas_call(
        near_kernel,
        in_specs=[VM, VM],
        out_specs=VM,
        out_shape=jax.ShapeDtypeStruct((rows, rep.shape[0]), F32),
        cost_estimate=cost(rows, rep.shape[0], vocab),
        compiler_params=params(8),
        name="near",
    )(rep, block)


def pair_kernel(fold, rep, mix, rank, first, *refs):
    queries, out = refs[:-1], refs[-1]
    docs = mix.shape[1]
    lines = docs // fold
    paired = jnp.concatenate(
        [first[...]]
        + [
            lax.dot_general(
                block[...], rep[...], (((1,), (1,)), ((), ())), preferred_element_type=F32
            )
            for block in queries
        ],
        axis=0,
    )
    parts = jnp.dot(paired, mix[...], precision=HIGH, preferred_element_type=F32)
    line = iota((docs, 1), 0)
    chosen = (fold * (line % lines) + line // lines == rank[...]).astype(F32)
    ordered = jnp.dot(chosen, parts, precision=HIGH, preferred_element_type=F32)
    columns = [ordered[m * lines : (m + 1) * lines, :] for m in range(fold)]
    packed = columns[0] if fold == 1 else jnp.concatenate(columns, axis=1)
    for k in range(out.shape[0]):
        out[k] = packed


def pair(blocks, rep, mix, rank, fold, copies):
    docs = mix.shape[1]
    return pl.pallas_call(
        functools.partial(pair_kernel, fold),
        in_specs=[VM] * (3 + len(blocks)),
        out_specs=VM,
        out_shape=jax.ShapeDtypeStruct((copies, docs // fold, docs * fold), F32),
        compiler_params=params(8),
        name="pair",
    )(rep, mix, rank, near(blocks[0], rep), *blocks[1:])


def backward_kernel(fold, spans, width, first, parts, mix, rank, slope, kept_slope, weight, *refs):
    queries, (scores, dlogit, token, held, sem, slope_sem) = refs[:-6], refs[-6:]
    loads = []
    for j, (begin, n) in enumerate(spans):
        at = pl.ds(begin, n)
        pair_of = [pltpu.make_async_copy(weight.at[pl.ds(0, width), at], held.at[:, at], sem.at[j])]
        if begin < slope.shape[1]:
            pair_of.append(
                pltpu.make_async_copy(slope.at[:, at], dlogit.at[:, at], slope_sem.at[j])
            )
        loads.append(pair_of)
    for pair_of in loads[:AHEAD]:
        for load in pair_of:
            load.start()
    vocab = weight.shape[1]
    rows, docs = mix.shape
    lines = docs // fold
    packed = parts[0]
    for k in range(1, parts.shape[0]):
        packed = packed + parts[k]
    folded = [packed[:, m * docs : (m + 1) * docs] for m in range(fold)]
    score = folded[0] if fold == 1 else jnp.concatenate(folded, axis=0)
    line = iota((docs, 1), 0)
    row = fold * (line % lines) + line // lines
    for k in range(scores.shape[0]):
        scores[k : k + 1, :] = jnp.sum(
            jnp.where(row == first[0] + k, score, 0.0), axis=0, keepdims=True
        )
    top = jnp.max(score, axis=1, keepdims=True)
    raised = jnp.exp(score - top)
    prob = raised / jnp.sum(raised, axis=1, keepdims=True)
    target = (iota((docs, docs), 1) == row).astype(F32)
    dscore = (prob - target) / docs
    by_line = lax.dot_general(
        mix[...], dscore, (((1,), (1,)), ((), ())), precision=HIGH, preferred_element_type=F32
    )
    place = (row == rank[...]).astype(F32)
    factor = jnp.dot(by_line, place, precision=HIGH, preferred_element_type=F32)
    upper = factor.astype(BF16)
    lower = (factor - upper.astype(F32)).astype(BF16)
    both = jnp.concatenate([upper, lower], axis=1)
    total = None
    for j, (begin, n) in enumerate(spans):
        at = pl.ds(begin, n)
        part = [block[:, at] for block in queries]
        drep = jnp.dot(both, jnp.concatenate(part + part, axis=0), preferred_element_type=F32)
        for load in loads[j]:
            load.wait()
        if j + AHEAD < len(loads):
            for load in loads[j + AHEAD]:
                load.start()
        for t in range(slope.shape[0] // rows):
            block = slice(t * rows, (t + 1) * rows)
            if begin < slope.shape[1]:
                steep = dlogit[block, at]
            else:
                steep = kept_slope[block, pl.ds(begin - slope.shape[1], n)]
            dlogit[block, at] = (steep.astype(F32) * drep).astype(BF16)
        add = lax.dot_general(
            dlogit[:, at], held[:, at], (((1,), (1,)), ((), ())), preferred_element_type=F32
        )
        total = add if j == 0 else total + add
    token[...] = total.astype(BF16)


def backward(parts, mix, rank, first, blocks, slope, kept_slope, weight, fold, owned, width):
    rows, docs = mix.shape
    cells = slope.shape[0]
    vocab = weight.shape[1]
    out = slope.shape[1]
    spans = ((out, vocab - out),) + spans_of(out, BACKWARD)
    return pl.pallas_call(
        functools.partial(backward_kernel, fold, spans, width),
        in_specs=[pl.BlockSpec(memory_space=pltpu.SMEM)] + [VM] * 3 + [HBM, VM, HBM]
        + [VM] * len(blocks),
        out_specs=[VM, VM, VM],
        out_shape=[
            jax.ShapeDtypeStruct((owned, docs), F32),
            pltpu.VMEM((cells, vocab), BF16),
            jax.ShapeDtypeStruct((cells, width), BF16),
        ],
        scratch_shapes=[
            pltpu.VMEM((width, vocab), BF16),
            pltpu.SemaphoreType.DMA((len(spans),)),
            pltpu.SemaphoreType.DMA((len(spans),)),
        ],
        cost_estimate=cost(cells, width, vocab),
        compiler_params=params(32),
        name="backward",
    )(first, parts, mix, rank, in_hbm(slope), kept_slope, in_hbm(weight), *blocks)


def cost(cells, width, vocab):
    return pl.CostEstimate(
        flops=2 * cells * width * vocab,
        transcendentals=0,
        bytes_accessed=2 * width * vocab + 2 * cells * vocab,
    )


def rest_kernel(begin, spans, dlogit, weight, token, held, sem):
    width = token.shape[1]
    loads = []
    for j, (first, n) in enumerate(spans):
        at = pl.ds(first, n)
        loads.append(
            pltpu.make_async_copy(weight.at[pl.ds(begin, width), at], held.at[:, at], sem.at[j])
        )
    for load in loads[:AHEAD]:
        load.start()
    total = None
    for j, load in enumerate(loads):
        at = pl.ds(*spans[j])
        load.wait()
        if j + AHEAD < len(loads):
            loads[j + AHEAD].start()
        add = lax.dot_general(
            dlogit[:, at], held[:, at], (((1,), (1,)), ((), ())), preferred_element_type=F32
        )
        total = add if j == 0 else total + add
    token[...] = total.astype(BF16)


def rest(dlogit, weight, begin, width):
    cells, vocab = dlogit.shape
    spans = spans_of(vocab, REST)
    return pl.pallas_call(
        functools.partial(rest_kernel, begin, spans),
        in_specs=[VM, HBM],
        out_specs=VM,
        out_shape=jax.ShapeDtypeStruct((cells, width), BF16),
        scratch_shapes=[
            pltpu.VMEM((width, vocab), BF16),
            pltpu.SemaphoreType.DMA((len(spans),)),
        ],
        cost_estimate=cost(cells, width, vocab),
        compiler_params=params(32),
        name="rest",
    )(dlogit, in_hbm(weight))


def place_kernel(copies, begin, positions, *refs):
    tokens, (out, made, sem) = refs[:copies], refs[-3:]
    picks, rows = positions.shape
    slots, width = made.shape
    seq = slots // rows
    cells = positions[...] + seq * iota((picks, rows), 1)
    target = jnp.concatenate([cells[t : t + 1, :] for t in range(picks)], axis=1)
    spread = (iota((slots, rows * picks), 0) == target).astype(F32).astype(BF16)
    total = None
    for ref in tokens:
        part = jnp.dot(spread, ref[...], preferred_element_type=F32)
        total = part if total is None else total + part
    made[...] = total.astype(BF16)
    copy = pltpu.make_async_copy(made, out.at[:, pl.ds(begin, width)], sem)
    copy.start()
    copy.wait()


def place(positions, tokens, begin, before, slots, width):
    part = tokens[0].shape[1]
    given = [] if before is None else [before]
    return pl.pallas_call(
        functools.partial(place_kernel, len(tokens), begin),
        in_specs=[VM] * (1 + len(tokens)) + [HBM] * len(given),
        out_specs=HBM,
        out_shape=pltpu.HBM((slots, width), BF16),
        scratch_shapes=[pltpu.VMEM((slots, part), BF16), pltpu.SemaphoreType.DMA(())],
        input_output_aliases={1 + len(tokens): 0} if given else {},
        cost_estimate=cost(slots, part, tokens[0].shape[0]),
        compiler_params=params(8),
        name="place",
    )(positions, *tokens, *given)


def on_device(sizes, hidden, positions, weight, counts, slots, head_weight, head_bias, queries):
    rows, seq, width = hidden.shape
    docs = counts.shape[0]
    owned, vocab = queries.shape
    fold = max(1, 128 // docs)
    vocs = sizes["voc"]
    axes = ("outer", "inner", "core")
    here = lax.axis_index(axes)
    first_slot = (here * rows).astype(jnp.int32).reshape(1)
    first_query = (here * owned).astype(jnp.int32).reshape(1)
    spots = positions.T
    around = sizes["outer"] * sizes["inner"]
    lead = 256
    sent, picked, mix, shift, lead_weight = ready(
        first_slot, queries, hidden, spots, slots, counts, weight, head_bias, head_weight,
        around, lead,
    )
    spread = lax.all_to_all(sent, ("outer", "inner"), 0, 0)
    rank = query_ranks(owned, sizes)
    slope, kept_slope, rep = forward(picked, shift, lead_weight, head_weight, rows)
    spread, rep = lax.optimization_barrier((spread, rep))
    blocks = join_queries(spread.reshape(-1, vocab), sizes["core"])
    everyone = sizes["outer"] * sizes["inner"] * sizes["core"] * vocs
    if everyone * docs * docs * 4 <= MIB:
        parts = pair(blocks, rep, mix, rank, fold, everyone)
        parts = lax.all_to_all(parts, axes + ("voc",), 0, 0)
    else:
        parts = pair(blocks, rep, mix, rank, fold, 1)
        parts = lax.psum(parts, axes + ("voc",))
    cut = width // 3 * 2 if width % 384 == 0 else width
    scores, dlogit, token = backward(
        parts, mix, rank, first_query, blocks, slope, kept_slope, head_weight,
        fold, owned, cut,
    )
    pieces = [token]
    if cut < width:
        pieces.append(rest(dlogit, head_weight, cut, width - cut))
    grad, begin = None, 0
    for token in pieces:
        if vocs == 2:
            tokens = [token, lax.ppermute(token, "voc", [(0, 1), (1, 0)])]
        else:
            tokens = [lax.psum(token, "voc")]
        grad = place(spots, tokens, begin, grad, rows * seq, width)
        begin += token.shape[1]
    return scores, grad.reshape(rows, seq, width)


def solution(mesh):
    outer, inner, core = grid_of(mesh.shape["pass"])
    sizes = {"outer": outer, "inner": inner, "core": core, "voc": mesh.shape["voc"]}
    fine = Mesh(mesh.devices.reshape(tuple(sizes.values())), tuple(sizes))
    whole = ("outer", "inner", "core")
    placed = (
        P(whole, None, None),
        P(whole, None),
        P(whole),
        P(),
        P(),
        P(None, "voc"),
        P("voc"),
        P(whole, "voc"),
    )
    return jax.shard_map(
        functools.partial(on_device, sizes),
        mesh=fine,
        in_specs=placed,
        out_specs=(P(whole, None), P(whole, None, None)),
        check_vma=False,
    )
```
